32 devices in a mesh: space: 16 (over z, y, x), tm: 2 (over core).
Axes of the slice: x: 2, y: 2, z: 4, core: 2. Of those that a mesh axis runs over, the one named last changes fastest.
Arguments:
- snapshots: bfloat16 [131072, 128], P('space', 'tm'), may hold values from -6 to 6
- basis: bfloat16 [131072, 192], P('space'), may hold values from -0.015625 to 0.015625
- tile_slots: int32 [704], P(('space', 'tm')), may hold values from 0 to 703, each once
Outputs:
- gram_tiles: float32 [704, 512, 512], P(('space', 'tm'))
The draws below stay inside these ranges and needn't reach their ends.
Inputs may be any that keep to these rules, and one draw needn't show every extreme that they name: `tile_slots`: every tile number below 703 stands in exactly one slot; the other values mark empty slots.
All inputs are finite; a program needn't handle non-finite values.
Results may differ from the reference program's by a relative error of at most 0.0039.
Values sent between devices are 32-bit elements; how exact they have to be, the bound alone decides.
A program may use at most 128 MiB of HBM per device.

```python
import jax
import jax.numpy as jnp
import numpy as np
from jax import lax

R = 192
BLK = 512
NCELL = 131072
NT = 128
NB = 37
NTILE = 703
SLOTS = 22
DEVICES = 32


def levels(own_key, extent, split, least, top_value):
    loudness, own = 1.0, jax.random.fold_in(own_key, 6)
    for axis_at, blocks in split:
        draws = jnp.exp(jax.random.uniform(jax.random.fold_in(own, axis_at), (blocks,), jnp.float32, least / len(split), top_value / len(split)))
        loudness = loudness * jnp.repeat(draws, extent[axis_at] // blocks).reshape([-1 if axis == axis_at else 1 for axis in range(len(extent))])
    return loudness


def bell_draw(key, shape, scale, most, split=(), kind=jnp.bfloat16):
    level = levels(key, shape, split, -0.22, 0.18) if split else 1.0
    entries = jax.random.normal(key, shape, jnp.float32) * scale * level
    return jnp.minimum(jnp.maximum(entries, -most), most).astype(kind)


def setup_inputs(seed: int = 0) -> dict:
    splits = jax.random.split(jax.random.key(seed), 4)
    return {
        "snapshots": bell_draw(splits[0], (NCELL, NT), 1.0, 6.0, ((0, 16), (1, 2))),
        "basis": bell_draw(splits[1], (NCELL, R), NCELL ** -0.5, 0.015625, ((0, 16),)),
        "tile_slots": jax.random.permutation(splits[2], DEVICES * SLOTS).astype(jnp.int32),
    }


def pair_tables():
    first = []
    second = []
    for k in range(R):
        first.append(k)
        second.append(R)
    for i in range(R):
        for j in range(i, R):
            first.append(i)
            second.append(j)
    while len(first) < NB * BLK:
        first.append(R + 1)
        second.append(R + 1)
    return np.array(first, dtype=np.int32), np.array(second, dtype=np.int32)


def tile_tables():
    rows_list = []
    cols_list = []
    for a in range(NB):
        for b in range(a + 1):
            rows_list.append(a)
            cols_list.append(b)
    return np.array(rows_list, dtype=np.int32), np.array(cols_list, dtype=np.int32)


def reference(snapshots, basis, tile_slots):
    coeffs = jnp.dot(basis.T, snapshots, preferred_element_type=jnp.float32)
    count = coeffs.shape[1]
    extended = jnp.concatenate([coeffs, jnp.ones((1, count), jnp.float32), jnp.zeros((1, count), jnp.float32)], axis=0)
    first, second = pair_tables()
    feats = (extended[jnp.asarray(first)] * extended[jnp.asarray(second)]).astype(jnp.bfloat16)
    feats = lax.optimization_barrier(feats).astype(jnp.float32).reshape(NB, BLK, count)
    tile_row, tile_col = tile_tables()
    tile_row = jnp.asarray(tile_row)
    tile_col = jnp.asarray(tile_col)

    def one_slot(slot):
        valid = (slot < NTILE).astype(jnp.float32)
        index = jnp.minimum(slot, NTILE - 1)
        left = feats[tile_row[index]]
        right = feats[tile_col[index]]
        block = jnp.dot(left, right.T, precision=lax.Precision.HIGHEST)
        return block * (valid / count)

    return lax.map(one_slot, tile_slots)
```

```python
import functools

import jax
import jax.numpy as jnp
from jax import lax
from jax.experimental import pallas as pl
from jax.experimental.pallas import tpu as pltpu
from jax.sharding import PartitionSpec as P

R = 192
BLK = 512
NB = 37
NTILE = NB * (NB + 1) // 2
HALF = R // 2
LANES = 128
MESH = pl.DeviceIdType.MESH

NT_DIMS = (((1,), (1,)), ((), ()))


def segment_starts():
    starts, at = [], R
    for i in range(R):
        starts.append(at)
        at += R - i
    return starts, at


def coeff_kernel(
    n, tm, chunks, basis_ref, snap_ref, out_ref,
    bas, snp, whole, part, recv, gath, flat,
    bas_sem, snp_sem, send1, recv1, send2, recv2,
):
    total = n * tm
    s = lax.axis_index("space")
    t = lax.axis_index("tm")
    me = s * tm + t
    width = snap_ref.shape[0]
    depth = basis_ref.shape[1] // chunks
    rows = HALF // n

    loads = []
    for k in range(chunks):
        at = pl.ds(k * depth, depth)
        one = pltpu.make_async_copy(basis_ref.at[:, at], bas.at[k], bas_sem.at[k])
        two = pltpu.make_async_copy(snap_ref.at[:, at], snp.at[k], snp_sem.at[k])
        one.start()
        two.start()
        loads.append((one, two))

    barrier = pltpu.get_barrier_semaphore()

    def greet(d, carry):
        peer = lax.rem(me + d, total)
        pl.semaphore_signal(
            barrier, inc=1,
            device_id={"space": lax.div(peer, tm), "tm": lax.rem(peer, tm)},
            device_id_type=MESH,
        )
        return carry

    lax.fori_loop(1, total, greet, 0)

    acc = jnp.zeros((R, width), jnp.float32)
    for k in range(chunks):
        loads[k][0].wait()
        loads[k][1].wait()
        acc = acc + lax.dot_general(
            bas[k], snp[k], NT_DIMS, preferred_element_type=jnp.float32
        )
    whole[...] = jnp.concatenate([acc[:HALF], acc[HALF:]], axis=1)
    for q in range(n):
        part[q] = whole[q * rows:(q + 1) * rows, :]

    pl.semaphore_wait(barrier, total - 1)

    def scatter(d):
        dst = lax.rem(s + d, n)
        return pltpu.make_async_remote_copy(
            src_ref=part.at[dst], dst_ref=recv.at[d],
            send_sem=send1.at[d], recv_sem=recv1.at[d],
            device_id={"space": dst, "tm": t}, device_id_type=MESH,
        )

    def start_scatter(d, carry):
        scatter(d).start()
        return carry

    lax.fori_loop(1, n, start_scatter, 0)

    def add(d, value):
        scatter(d).wait_recv()
        return value + recv[d]

    gath[t, s] = lax.fori_loop(1, n, add, part[s])

    def gather(d):
        peer = lax.rem(me + d, total)
        return pltpu.make_async_remote_copy(
            src_ref=gath.at[t, s], dst_ref=gath.at[t, s],
            send_sem=send2.at[d], recv_sem=recv2.at[d],
            device_id={"space": lax.div(peer, tm), "tm": lax.rem(peer, tm)},
            device_id_type=MESH,
        )

    def start_gather(d, carry):
        gather(d).start()
        return carry

    lax.fori_loop(1, total, start_gather, 0)

    def end_scatter(d, carry):
        scatter(d).wait_send()
        return carry

    lax.fori_loop(1, n, end_scatter, 0)

    def end_gather(d, carry):
        gather(d).wait_recv()
        return carry

    lax.fori_loop(1, total, end_gather, 0)

    for u in range(tm):
        for q in range(n):
            flat[u, q * rows:(q + 1) * rows, :] = gath[u, q]
    per = LANES // width
    for v in range(tm // per):
        blocks = [flat[v * per + u] for u in range(per)]
        for h in range(2):
            out_ref[v, h * HALF:(h + 1) * HALF, :] = jnp.concatenate(
                [b[:, h * width:(h + 1) * width] for b in blocks], axis=1
            )

    def end_send(d, carry):
        gather(d).wait_send()
        return carry

    lax.fori_loop(1, total, end_send, 0)


def coefficients(n, tm, basis_t, snap_t):
    width, cells = snap_t.shape
    chunks = 4
    depth = cells // chunks
    total = n * tm
    rows = HALF // n
    blocks = tm * width // LANES
    return pl.pallas_call(
        functools.partial(coeff_kernel, n, tm, chunks),
        out_shape=jax.ShapeDtypeStruct((blocks, R, LANES), jnp.float32),
        in_specs=[pl.BlockSpec(memory_space=pl.ANY)] * 2,
        out_specs=pl.BlockSpec(memory_space=pltpu.VMEM),
        scratch_shapes=[
            pltpu.VMEM((chunks, R, depth), jnp.bfloat16),
            pltpu.VMEM((chunks, width, depth), jnp.bfloat16),
            pltpu.VMEM((HALF, LANES), jnp.float32),
            pltpu.VMEM((n, rows, LANES), jnp.float32),
            pltpu.VMEM((n, rows, LANES), jnp.float32),
            pltpu.VMEM((tm, n, rows, LANES), jnp.float32),
            pltpu.VMEM((tm, HALF, LANES), jnp.float32),
            pltpu.SemaphoreType.DMA((chunks,)),
            pltpu.SemaphoreType.DMA((chunks,)),
            pltpu.SemaphoreType.DMA((n,)),
            pltpu.SemaphoreType.DMA((n,)),
            pltpu.SemaphoreType.DMA((total,)),
            pltpu.SemaphoreType.DMA((total,)),
        ],
        compiler_params=pltpu.CompilerParams(collective_id=0, has_side_effects=True),
        name="coeffs",
    )(basis_t, snap_t)


def tile_kernel(slots_ref, coeff_ref, out_ref, wide, feats, tiles, sems):
    blocks = coeff_ref.shape[0]
    slots = out_ref.shape[0]
    steps = blocks * LANES
    starts, end = segment_starts()

    for v in range(blocks):
        wide[v, :R, :] = coeff_ref[v]
        wide[v, R:, :] = jnp.zeros((8, LANES), jnp.float32)
        feats[v, end:, :] = jnp.zeros((feats.shape[1] - end, LANES), jnp.float32)

    @pl.loop(0, blocks)
    def _(v):
        feats[v, :R, :] = wide[v, :R, :]
        for i in range(R):
            size = R - i
            feats[v, starts[i]:starts[i] + size, :] = (
                wide[v, i:i + size, :] * wide[v, i:i + 1, :]
            )

    def copy(k):
        return pltpu.make_async_copy(tiles.at[k], out_ref.at[k], sems.at[k])

    @pl.loop(0, slots)
    def _(k):
        slot = slots_ref[k]
        index = jnp.minimum(slot, NTILE - 1)
        a = jnp.int32(0)
        for m in range(1, NB):
            a = a + (index >= m * (m + 1) // 2).astype(jnp.int32)
        b = index - lax.div(a * (a + 1), 2)
        scale = jnp.where(slot < NTILE, jnp.float32(1.0 / steps), jnp.float32(0.0))
        left_at = pl.ds(pl.multiple_of(a * BLK, BLK), BLK)
        right_at = pl.ds(pl.multiple_of(b * BLK, BLK), BLK)
        out = None
        for v in range(blocks):
            left = feats[v, left_at, :].astype(jnp.bfloat16)
            right = feats[v, right_at, :].astype(jnp.bfloat16)
            one = lax.dot_general(left, right, NT_DIMS, preferred_element_type=jnp.float32)
            out = one if out is None else out + one
        tiles[k] = out * scale
        copy(k).start()

    @pl.loop(0, slots)
    def _(k):
        copy(k).wait()


def gram(tile_slots, coeffs):
    slots = tile_slots.shape[0]
    blocks = coeffs.shape[0]
    return pl.pallas_call(
        tile_kernel,
        out_shape=jax.ShapeDtypeStruct((slots, BLK, BLK), jnp.float32),
        in_specs=[
            pl.BlockSpec(memory_space=pltpu.SMEM),
            pl.BlockSpec(memory_space=pltpu.VMEM),
        ],
        out_specs=pl.BlockSpec(memory_space=pl.ANY),
        scratch_shapes=[
            pltpu.VMEM((blocks, R + 8, LANES), jnp.float32),
            pltpu.VMEM((blocks, NB * BLK, LANES), jnp.float32),
            pltpu.VMEM((slots, BLK, BLK), jnp.float32),
            pltpu.SemaphoreType.DMA((slots,)),
        ],
        compiler_params=pltpu.CompilerParams(vmem_limit_bytes=56 << 20),
        name="tiles",
    )(tile_slots, coeffs)


def body(n, tm, snapshots, basis, tile_slots):
    coeffs = coefficients(n, tm, basis.T, snapshots.T)
    return gram(tile_slots, coeffs)


def solution(mesh):
    n, tm = mesh.shape["space"], mesh.shape["tm"]
    in_specs = (P("space", "tm"), P("space", None), P(("space", "tm")))
    out_specs = P(("space", "tm"), None, None)
    return jax.shard_map(
        functools.partial(body, n, tm), mesh=mesh,
        in_specs=in_specs, out_specs=out_specs, check_vma=False,
    )
```

```python
import functools

import jax
import jax.numpy as jnp
from jax import lax
from jax.experimental import pallas as pl
from jax.experimental.pallas import tpu as pltpu
from jax.sharding import PartitionSpec as P

R = 192
BLK = 512
NB = 37
NTILE = NB * (NB + 1) // 2
HALF = R // 2
LANES = 128
MESH = pl.DeviceIdType.MESH

NT_DIMS = (((1,), (1,)), ((), ()))


def segment_starts():
    starts, at = [], R
    for i in range(R):
        starts.append(at)
        at += R - i
    return starts, at


def coeff_kernel(
    n, tm, chunks, basis_ref, snap_ref, out_ref,
    bas, snp, whole, part, recv, gath, flat,
    bas_sem, snp_sem, send1, recv1, send2, recv2,
):
    total = n * tm
    s = lax.axis_index("space")
    t = lax.axis_index("tm")
    me = s * tm + t
    width = snap_ref.shape[0]
    depth = basis_ref.shape[1] // chunks
    rows = HALF // n

    loads = []
    for k in range(chunks):
        at = pl.ds(k * depth, depth)
        one = pltpu.make_async_copy(basis_ref.at[:, at], bas.at[k], bas_sem.at[k])
        two = pltpu.make_async_copy(snap_ref.at[:, at], snp.at[k], snp_sem.at[k])
        one.start()
        two.start()
        loads.append((one, two))

    barrier = pltpu.get_barrier_semaphore()

    def greet(d, carry):
        peer = lax.rem(me + d, total)
        pl.semaphore_signal(
            barrier, inc=1,
            device_id={"space": lax.div(peer, tm), "tm": lax.rem(peer, tm)},
            device_id_type=MESH,
        )
        return carry

    lax.fori_loop(1, total, greet, 0)

    acc = jnp.zeros((R, width), jnp.float32)
    for k in range(chunks):
        loads[k][0].wait()
        loads[k][1].wait()
        acc = acc + lax.dot_general(
            bas[k], snp[k], NT_DIMS, preferred_element_type=jnp.float32
        )
    whole[...] = jnp.concatenate([acc[:HALF], acc[HALF:]], axis=1)
    for q in range(n):
        part[q] = whole[q * rows:(q + 1) * rows, :]

    pl.semaphore_wait(barrier, total - 1)

    def scatter(d):
        dst = lax.rem(s + d, n)
        return pltpu.make_async_remote_copy(
            src_ref=part.at[dst], dst_ref=recv.at[d],
            send_sem=send1.at[d], recv_sem=recv1.at[d],
            device_id={"space": dst, "tm": t}, device_id_type=MESH,
        )

    def start_scatter(d, carry):
        scatter(d).start()
        return carry

    lax.fori_loop(1, n, start_scatter, 0)

    def add(d, value):
        scatter(d).wait_recv()
        return value + recv[d]

    gath[t, s] = lax.fori_loop(1, n, add, part[s])

    def gather(d):
        peer = lax.rem(me + d, total)
        return pltpu.make_async_remote_copy(
            src_ref=gath.at[t, s], dst_ref=gath.at[t, s],
            send_sem=send2.at[d], recv_sem=recv2.at[d],
            device_id={"space": lax.div(peer, tm), "tm": lax.rem(peer, tm)},
            device_id_type=MESH,
        )

    def start_gather(d, carry):
        gather(d).start()
        return carry

    lax.fori_loop(1, total, start_gather, 0)

    def end_scatter(d, carry):
        scatter(d).wait_send()
        return carry

    lax.fori_loop(1, n, end_scatter, 0)

    def end_gather(d, carry):
        gather(d).wait_recv()
        return carry

    lax.fori_loop(1, total, end_gather, 0)

    for u in range(tm):
        for q in range(n):
            flat[u, q * rows:(q + 1) * rows, :] = gath[u, q]
    per = LANES // width
    for v in range(tm // per):
        blocks = [flat[v * per + u] for u in range(per)]
        for h in range(2):
            out_ref[v, h * HALF:(h + 1) * HALF, :] = jnp.concatenate(
                [b[:, h * width:(h + 1) * width] for b in blocks], axis=1
            )

    def end_send(d, carry):
        gather(d).wait_send()
        return carry

    lax.fori_loop(1, total, end_send, 0)


def coefficients(n, tm, basis_t, snap_t):
    width, cells = snap_t.shape
    chunks = 2
    depth = cells // chunks
    total = n * tm
    rows = HALF // n
    blocks = tm * width // LANES
    return pl.pallas_call(
        functools.partial(coeff_kernel, n, tm, chunks),
        out_shape=pltpu.VMEM((blocks, R, LANES), jnp.float32),
        in_specs=[pl.BlockSpec(memory_space=pl.ANY)] * 2,
        out_specs=pl.BlockSpec(memory_space=pltpu.VMEM),
        scratch_shapes=[
            pltpu.VMEM((chunks, R, depth), jnp.bfloat16),
            pltpu.VMEM((chunks, width, depth), jnp.bfloat16),
            pltpu.VMEM((HALF, LANES), jnp.float32),
            pltpu.VMEM((n, rows, LANES), jnp.float32),
            pltpu.VMEM((n, rows, LANES), jnp.float32),
            pltpu.VMEM((tm, n, rows, LANES), jnp.float32),
            pltpu.VMEM((tm, HALF, LANES), jnp.float32),
            pltpu.SemaphoreType.DMA((chunks,)),
            pltpu.SemaphoreType.DMA((chunks,)),
            pltpu.SemaphoreType.DMA((n,)),
            pltpu.SemaphoreType.DMA((n,)),
            pltpu.SemaphoreType.DMA((total,)),
            pltpu.SemaphoreType.DMA((total,)),
        ],
        compiler_params=pltpu.CompilerParams(collective_id=0, has_side_effects=True),
        name="coeffs",
    )(basis_t, snap_t)


def tile_kernel(slots_ref, coeff_ref, out_ref, wide, feats, tiles, sems):
    blocks = coeff_ref.shape[0]
    slots = out_ref.shape[0]
    steps = blocks * LANES
    starts, end = segment_starts()

    for v in range(blocks):
        wide[v, :R, :] = coeff_ref[v]
        wide[v, R:, :] = jnp.zeros((8, LANES), jnp.float32)
        feats[v, end:, :] = jnp.zeros((feats.shape[1] - end, LANES), jnp.float32)

    @pl.loop(0, blocks)
    def _(v):
        feats[v, :R, :] = wide[v, :R, :]
        for i in range(R):
            size = R - i
            feats[v, starts[i]:starts[i] + size, :] = (
                wide[v, i:i + size, :] * wide[v, i:i + 1, :]
            )

    def copy(k):
        return pltpu.make_async_copy(tiles.at[k], out_ref.at[k], sems.at[k])

    @pl.loop(0, slots, unroll=2 if slots % 2 == 0 else 1)
    def _(k):
        slot = slots_ref[k]
        index = jnp.minimum(slot, NTILE - 1)
        a = jnp.int32(0)
        for m in range(1, NB):
            a = a + (index >= m * (m + 1) // 2).astype(jnp.int32)
        b = index - lax.div(a * (a + 1), 2)
        scale = jnp.where(slot < NTILE, jnp.float32(1.0 / steps), jnp.float32(0.0))
        left_at = pl.ds(pl.multiple_of(a * BLK, BLK), BLK)
        right_at = pl.ds(pl.multiple_of(b * BLK, BLK), BLK)
        out = None
        for v in range(blocks):
            left = feats[v, left_at, :].astype(jnp.bfloat16)
            right = feats[v, right_at, :].astype(jnp.bfloat16)
            one = lax.dot_general(left, right, NT_DIMS, preferred_element_type=jnp.float32)
            out = one if out is None else out + one
        tiles[k] = out * scale
        copy(k).start()

    @pl.loop(0, slots)
    def _(k):
        copy(k).wait()


def gram(tile_slots, coeffs):
    slots = tile_slots.shape[0]
    blocks = coeffs.shape[0]
    return pl.pallas_call(
        tile_kernel,
        out_shape=jax.ShapeDtypeStruct((slots, BLK, BLK), jnp.float32),
        in_specs=[
            pl.BlockSpec(memory_space=pltpu.SMEM),
            pl.BlockSpec(memory_space=pltpu.VMEM),
        ],
        out_specs=pl.BlockSpec(memory_space=pl.ANY),
        scratch_shapes=[
            pltpu.VMEM((blocks, R + 8, LANES), jnp.float32),
            pltpu.VMEM((blocks, NB * BLK, LANES), jnp.float32),
            pltpu.VMEM((slots, BLK, BLK), jnp.float32),
            pltpu.SemaphoreType.DMA((slots,)),
        ],
        compiler_params=pltpu.CompilerParams(vmem_limit_bytes=56 << 20),
        name="tiles",
    )(
        pltpu.with_memory_space_constraint(tile_slots, pltpu.HBM),
        pltpu.with_memory_space_constraint(coeffs, pltpu.VMEM),
    )


def body(n, tm, snapshots, basis, tile_slots):
    coeffs = coefficients(n, tm, basis.T, snapshots.T)
    return gram(tile_slots, coeffs)


def solution(mesh):
    n, tm = mesh.shape["space"], mesh.shape["tm"]
    in_specs = (P("space", "tm"), P("space", None), P(("space", "tm")))
    out_specs = P(("space", "tm"), None, None)
    return jax.shard_map(
        functools.partial(body, n, tm), mesh=mesh,
        in_specs=in_specs, out_specs=out_specs, check_vma=False,
    )
```

```python
import functools

import jax
import jax.numpy as jnp
from jax import lax
from jax.experimental import pallas as pl
from jax.experimental.pallas import tpu as pltpu
from jax.sharding import PartitionSpec as P

R = 192
BLK = 512
NB = 37
NTILE = NB * (NB + 1) // 2
HALF = R // 2
LANES = 128
MESH = pl.DeviceIdType.MESH

NT_DIMS = (((1,), (1,)), ((), ()))


def segment_starts():
    starts, at = [], R
    for i in range(R):
        starts.append(at)
        at += R - i
    return starts, at


def coeff_kernel(
    n, tm, chunks, basis_ref, snap_ref, out_ref,
    bas, snp, whole, part, recv, gath, flat,
    bas_sem, snp_sem, send1, recv1, send2, recv2,
):
    total = n * tm
    s = lax.axis_index("space")
    t = lax.axis_index("tm")
    width = snap_ref.shape[0]
    depth = basis_ref.shape[1] // chunks
    rows = HALF // n

    loads = []
    for k in range(chunks):
        at = pl.ds(k * depth, depth)
        one = pltpu.make_async_copy(basis_ref.at[:, at], bas.at[k], bas_sem.at[k])
        two = pltpu.make_async_copy(snap_ref.at[:, at], snp.at[k], snp_sem.at[k])
        one.start()
        two.start()
        loads.append((one, two))

    def turn(v, size):
        return jnp.where(v >= size, v - size, v)

    spaces = [s] + [turn(s + d, n) for d in range(1, n)]
    times = [t] + [turn(t + e, tm) for e in range(1, tm)]
    peers = [{"space": p, "tm": u} for u in times for p in spaces]
    barrier = pltpu.get_barrier_semaphore()
    for peer in peers[1:]:
        pl.semaphore_signal(barrier, inc=1, device_id=peer, device_id_type=MESH)

    acc = jnp.zeros((R, width), jnp.float32)
    for k in range(chunks):
        loads[k][0].wait()
        loads[k][1].wait()
        acc = acc + lax.dot_general(
            bas[k], snp[k], NT_DIMS, preferred_element_type=jnp.float32
        )
    whole[...] = jnp.concatenate([acc[:HALF], acc[HALF:]], axis=1)
    for q in range(n):
        part[q] = whole[q * rows:(q + 1) * rows, :]

    pl.semaphore_wait(barrier, total - 1)

    scatters = [
        pltpu.make_async_remote_copy(
            src_ref=part.at[spaces[d]], dst_ref=recv.at[d],
            send_sem=send1.at[d], recv_sem=recv1.at[d],
            device_id=peers[d], device_id_type=MESH,
        )
        for d in range(1, n)
    ]
    for one in scatters:
        one.start()
    value = part[s]
    for d, one in enumerate(scatters):
        one.wait_recv()
        value = value + recv[d + 1]
    gath[t, s] = value

    gathers = [
        pltpu.make_async_remote_copy(
            src_ref=gath.at[t, s], dst_ref=gath.at[t, s],
            send_sem=send2.at[d], recv_sem=recv2.at[d],
            device_id=peers[d], device_id_type=MESH,
        )
        for d in range(1, total)
    ]
    for one in gathers:
        one.start()
    for one in scatters:
        one.wait_send()
    for one in gathers:
        one.wait_recv()

    for u in range(tm):
        for q in range(n):
            flat[u, q * rows:(q + 1) * rows, :] = gath[u, q]
    per = LANES // width
    for v in range(tm // per):
        blocks = [flat[v * per + u] for u in range(per)]
        for h in range(2):
            out_ref[v, h * HALF:(h + 1) * HALF, :] = jnp.concatenate(
                [b[:, h * width:(h + 1) * width] for b in blocks], axis=1
            )

    for one in gathers:
        one.wait_send()


def coefficients(n, tm, basis_t, snap_t):
    width, cells = snap_t.shape
    chunks = 2
    depth = cells // chunks
    total = n * tm
    rows = HALF // n
    blocks = tm * width // LANES
    return pl.pallas_call(
        functools.partial(coeff_kernel, n, tm, chunks),
        out_shape=pltpu.VMEM((blocks, R, LANES), jnp.float32),
        in_specs=[pl.BlockSpec(memory_space=pl.ANY)] * 2,
        out_specs=pl.BlockSpec(memory_space=pltpu.VMEM),
        scratch_shapes=[
            pltpu.VMEM((chunks, R, depth), jnp.bfloat16),
            pltpu.VMEM((chunks, width, depth), jnp.bfloat16),
            pltpu.VMEM((HALF, LANES), jnp.float32),
            pltpu.VMEM((n, rows, LANES), jnp.float32),
            pltpu.VMEM((n, rows, LANES), jnp.float32),
            pltpu.VMEM((tm, n, rows, LANES), jnp.float32),
            pltpu.VMEM((tm, HALF, LANES), jnp.float32),
            pltpu.SemaphoreType.DMA((chunks,)),
            pltpu.SemaphoreType.DMA((chunks,)),
            pltpu.SemaphoreType.DMA((n,)),
            pltpu.SemaphoreType.DMA((n,)),
            pltpu.SemaphoreType.DMA((total,)),
            pltpu.SemaphoreType.DMA((total,)),
        ],
        compiler_params=pltpu.CompilerParams(collective_id=0, has_side_effects=True),
        name="coeffs",
    )(basis_t, snap_t)


def tile_kernel(slots_ref, coeff_ref, out_ref, wide, feats, tiles, sems):
    blocks = coeff_ref.shape[0]
    slots = out_ref.shape[0]
    steps = blocks * LANES
    starts, end = segment_starts()

    for v in range(blocks):
        wide[v, :R, :] = coeff_ref[v]
        wide[v, R:, :] = jnp.zeros((8, LANES), jnp.float32)
        feats[v, end:, :] = jnp.zeros((feats.shape[1] - end, LANES), jnp.float32)

    @pl.loop(0, blocks)
    def _(v):
        feats[v, :R, :] = wide[v, :R, :]
        for i in range(R):
            size = R - i
            feats[v, starts[i]:starts[i] + size, :] = (
                wide[v, i:i + size, :] * wide[v, i:i + 1, :]
            )

    def copy(k):
        return pltpu.make_async_copy(tiles.at[k], out_ref.at[k], sems.at[k])

    @pl.loop(0, slots, unroll=2 if slots % 2 == 0 else 1)
    def _(k):
        slot = slots_ref[k]
        index = jnp.minimum(slot, NTILE - 1)
        a = jnp.int32(0)
        for m in range(1, NB):
            a = a + (index >= m * (m + 1) // 2).astype(jnp.int32)
        b = index - lax.div(a * (a + 1), 2)
        scale = jnp.where(slot < NTILE, jnp.float32(1.0 / steps), jnp.float32(0.0))
        left_at = pl.ds(pl.multiple_of(a * BLK, BLK), BLK)
        right_at = pl.ds(pl.multiple_of(b * BLK, BLK), BLK)
        out = None
        for v in range(blocks):
            left = feats[v, left_at, :].astype(jnp.bfloat16)
            right = feats[v, right_at, :].astype(jnp.bfloat16)
            one = lax.dot_general(left, right, NT_DIMS, preferred_element_type=jnp.float32)
            out = one if out is None else out + one
        tiles[k] = out * scale
        copy(k).start()

    @pl.loop(0, slots)
    def _(k):
        copy(k).wait()


def gram(tile_slots, coeffs):
    slots = tile_slots.shape[0]
    blocks = coeffs.shape[0]
    return pl.pallas_call(
        tile_kernel,
        out_shape=jax.ShapeDtypeStruct((slots, BLK, BLK), jnp.float32),
        in_specs=[
            pl.BlockSpec(memory_space=pltpu.SMEM),
            pl.BlockSpec(memory_space=pltpu.VMEM),
        ],
        out_specs=pl.BlockSpec(memory_space=pl.ANY),
        scratch_shapes=[
            pltpu.VMEM((blocks, R + 8, LANES), jnp.float32),
            pltpu.VMEM((blocks, NB * BLK, LANES), jnp.float32),
            pltpu.VMEM((slots, BLK, BLK), jnp.float32),
            pltpu.SemaphoreType.DMA((slots,)),
        ],
        compiler_params=pltpu.CompilerParams(vmem_limit_bytes=56 << 20),
        name="tiles",
    )(
        pltpu.with_memory_space_constraint(tile_slots, pltpu.HBM),
        pltpu.with_memory_space_constraint(coeffs, pltpu.VMEM),
    )


def body(n, tm, snapshots, basis, tile_slots):
    coeffs = coefficients(n, tm, basis.T, snapshots.T)
    return gram(tile_slots, coeffs)


def solution(mesh):
    n, tm = mesh.shape["space"], mesh.shape["tm"]
    in_specs = (P("space", "tm"), P("space", None), P(("space", "tm")))
    out_specs = P(("space", "tm"), None, None)
    return jax.shard_map(
        functools.partial(body, n, tm), mesh=mesh,
        in_specs=in_specs, out_specs=out_specs, check_vma=False,
    )
```
